256 devices in a mesh: tm: 8 (over x_hi, y), azim: 32 (over z, x_lo, core).
Axes of the slice: x: 4 (x_hi: 2, x_lo: 2; x = x_hi * 2 + x_lo), y: 4, z: 8, core: 2. Of those that a mesh axis runs over, the one named last changes fastest.
Arguments:
- rotor_coeffs: float32 [64, 2, 32, 16384], P('tm', None, 'azim'), may hold values from -1.5 to 1.5
- mortar_weights: float32 [64, 2, 32, 16384], P('tm', None, 'azim'), may hold values from 0.2 to 1
- block_shifts: int32 [64], P('tm'), may hold values from 0 to 31
- stencil_offsets: int32 [64, 2], P('tm'), may hold values from -1 to 1
- reluctivity: float32 [32, 16384], P('azim'), may hold values from 0.5 to 2
- source: float32 [64, 2, 32, 16384], P('tm', None, 'azim'), may hold values from -3 to 3
Outputs:
- residual: float32 [64, 2, 32, 16384], P('tm', None, 'azim')
The draws below stay inside these ranges and needn't reach their ends.
All inputs are finite; a program needn't handle non-finite values.
Results may differ from the reference program's by a relative error of at most 0.0001.
Values sent between devices are 32-bit elements; how exact they have to be, the bound alone decides.
A program may use at most 128 MiB of HBM per device.

```python
import math
import jax
import jax.numpy as jnp
from jax import lax

KC = 64
NT = 64
COMP = 2
STEN = 2
P_SIZE = 16384
NB = 32


def set_ends(entries, rng, low, top_value):
    place = [jax.random.randint(jax.random.fold_in(rng, axis), (), 0, length) for axis, length in enumerate(entries.shape)]
    main_axis = entries.shape.index(max(entries.shape))
    next_to = place[:main_axis] + [(place[main_axis] + 1) % entries.shape[main_axis]] + place[main_axis + 1:]
    return entries.at[tuple(place)].set(low).at[tuple(next_to)].set(top_value)


def levels(stream_key, dims, split, low, top_value):
    loudness = 1.0
    for dim, parts in split:
        draws = jax.random.uniform(jax.random.fold_in(jax.random.fold_in(stream_key, 6), dim), (parts,), jnp.float32, low / len(split), top_value / len(split))
        loudness = loudness * jnp.repeat(jnp.exp(draws), dims[dim] // parts).reshape((-1,) + (1,) * (len(dims) - 1 - dim))
    return loudness


def centred(rng, shape, scale, reach, pieces=(), kind=jnp.bfloat16):
    gain = levels(rng, shape, pieces, -0.22, 0.18) if pieces else 1.0
    array = jax.random.normal(rng, shape, jnp.float32) * scale * gain
    return jnp.minimum(jnp.maximum(array, -reach), reach).astype(kind)


def setup_inputs(seed: int = 0) -> dict:
    seeds = jax.random.split(jax.random.key(seed), 7)
    return {
        "rotor_coeffs": centred(seeds[0], (KC, COMP, NB, P_SIZE), 0.25, 1.5, ((0, 8), (2, 32)), jnp.float32),
        "mortar_weights": jnp.clip(0.2 + 0.8 * jax.random.uniform(seeds[1], (NT, STEN, NB, P_SIZE), jnp.float32) ** levels(seeds[1], (NT, STEN, NB, P_SIZE), ((0, 8), (2, 32)), -0.2, 0.2), 0.2, 1.0),
        "block_shifts": set_ends(jax.random.randint(seeds[2], (NT,), 0, NB), jax.random.fold_in(seeds[2], 1), 0, NB - 1).astype(jnp.int32),
        "stencil_offsets": set_ends(jax.random.randint(seeds[3], (NT, STEN), -1, 2), jax.random.fold_in(seeds[3], 1), -1, 1).astype(jnp.int32),
        "reluctivity": jnp.clip(jnp.exp(math.log(2.0) - 1.3862944 * jax.random.uniform(seeds[4], (NB, P_SIZE), jnp.float32) ** levels(seeds[4], (NB, P_SIZE), ((0, 32),), -0.2, 0.2)), 0.5, 2.0),
        "source": centred(seeds[5], (KC, COMP, NB, P_SIZE), 0.5, 3.0, ((0, 8), (2, 32)), jnp.float32),
    }


def harmonic_basis(sample_rows, coefficient_count):
    column = jnp.arange(coefficient_count, dtype=jnp.int32)
    harmonic_order = 2 * (column // 2) + 1
    phase_index = (harmonic_order[None, :] * (2 * sample_rows[:, None] + 1)) % (4 * NT)
    phase_angle = phase_index.astype(jnp.float32) * (jnp.pi / (2 * NT))
    return jnp.where(column[None, :] % 2 == 0, jnp.cos(phase_angle), jnp.sin(phase_angle))


def reference(rotor_coeffs, mortar_weights, block_shifts, stencil_offsets, reluctivity, source):
    basis_table = harmonic_basis(jnp.arange(NT, dtype=jnp.int32), KC)
    forward_scale = 2.0 / NT

    def one_sample(accumulated, inputs):
        basis_row, weights, shift_amount, offsets = inputs
        sample = jnp.tensordot(basis_row, rotor_coeffs, axes=(0, 0), precision=lax.Precision.HIGHEST)
        turned = jnp.roll(sample, shift_amount, axis=1)
        airgap_field = jnp.zeros_like(sample)
        for stencil_entry in range(STEN):
            airgap_field = airgap_field + weights[stencil_entry][None] * jnp.roll(turned, -offsets[stencil_entry], axis=1)
        square = jnp.sum(airgap_field * airgap_field, axis=0)
        field_flux = (reluctivity * (1.0 + square / (1.0 + square)))[None] * airgap_field
        accumulated = accumulated + forward_scale * basis_row[:, None, None, None] * field_flux[None]
        return accumulated, None

    start_value = jnp.zeros((KC, COMP, NB, P_SIZE), jnp.float32)
    accumulated, unused = lax.scan(one_sample, start_value, (basis_table, mortar_weights, block_shifts, stencil_offsets))
    return accumulated - source
```

```python
import jax
import jax.numpy as jnp
from jax import lax
from jax.sharding import PartitionSpec as P

KC = 64
NT = 64
LANES = 128


def shifted(value, axis, steps):
    count = lax.axis_size(axis)
    pairs = [(source, (source + steps) % count) for source in range(count)]
    return lax.ppermute(value, axis, pairs)


def harmonic_basis(sample_rows, coefficient_count):
    column = jnp.arange(coefficient_count, dtype=jnp.int32)
    harmonic_order = 2 * (column // 2) + 1
    phase_index = harmonic_order[None, :] * (2 * sample_rows[:, None] + 1) % (4 * NT)
    phase_angle = phase_index.astype(jnp.float32) * (jnp.pi / (2 * NT))
    return jnp.where(column[None, :] % 2 == 0, jnp.cos(phase_angle), jnp.sin(phase_angle))


def per_sample(flags, value):
    return flags.reshape((-1,) + (1,) * (value.ndim - 1))


def body(rotor_coeffs, mortar_weights, block_shifts, stencil_offsets, reluctivity, source):
    local_c, comp, _, nodes = rotor_coeffs.shape
    local_j, sten = mortar_weights.shape[:2]
    rows = nodes // LANES
    parts = lax.axis_size("tm")
    chunk = rows // parts
    coeffs = lax.all_to_all(
        rotor_coeffs.reshape(local_c, comp, rows, LANES), "tm", split_axis=2, concat_axis=0, tiled=True
    )
    weights = lax.all_to_all(
        mortar_weights.reshape(local_j, sten, rows, LANES), "tm", split_axis=2, concat_axis=0, tiled=True
    )
    shifts = lax.all_gather(block_shifts, "tm", tiled=True)
    offsets = lax.all_gather(stencil_offsets, "tm", tiled=True)
    gain = lax.dynamic_slice_in_dim(
        reluctivity.reshape(rows, LANES), lax.axis_index("tm") * chunk, chunk, axis=0
    )
    table = harmonic_basis(jnp.arange(NT, dtype=jnp.int32), KC)
    samples = jnp.einsum("jc,capk->japk", table, coeffs, precision=lax.Precision.HIGHEST)
    turned = samples
    for bit_level in range((lax.axis_size("azim") - 1).bit_length()):
        moved = shifted(turned, "azim", 1 << bit_level)
        chosen = (shifts >> bit_level) & 1 == 1
        turned = jnp.where(per_sample(chosen, turned), moved, turned)
    from_left = shifted(turned, "azim", 1)
    from_right = shifted(turned, "azim", -1)
    airgap_field = jnp.zeros_like(samples)
    for stencil_entry in range(sten):
        offset = offsets[:, stencil_entry]
        neighbour = jnp.where(
            per_sample(offset == 0, turned),
            turned,
            jnp.where(per_sample(offset > 0, turned), from_right, from_left),
        )
        airgap_field = airgap_field + weights[:, stencil_entry][:, None] * neighbour
    square = jnp.sum(airgap_field * airgap_field, axis=1, keepdims=True)
    field_flux = gain[None, None] * (1.0 + square / (1.0 + square)) * airgap_field
    summed = jnp.einsum(
        "jc,japk->capk", table * (2.0 / NT), field_flux, precision=lax.Precision.HIGHEST
    )
    residual = lax.all_to_all(summed, "tm", split_axis=0, concat_axis=2, tiled=True)
    return residual.reshape(source.shape) - source


def solution(mesh):
    in_specs = (
        P("tm", None, "azim", None),
        P("tm", None, "azim", None),
        P("tm"),
        P("tm", None),
        P("azim", None),
        P("tm", None, "azim", None),
    )
    out_specs = P("tm", None, "azim", None)
    return jax.shard_map(body, mesh=mesh, in_specs=in_specs, out_specs=out_specs, check_vma=False)
```

```python
import itertools

import jax
import jax.numpy as jnp
import numpy as np
from jax import lax
from jax.sharding import PartitionSpec as P

KC = 64
NT = 64
LANES = 128


def shifted(value, axis, steps):
    count = lax.axis_size(axis)
    pairs = [(source, (source + steps) % count) for source in range(count)]
    return lax.ppermute(value, axis, pairs)


def harmonic_basis(sample_rows, coefficient_count):
    column = jnp.arange(coefficient_count, dtype=jnp.int32)
    harmonic_order = 2 * (column // 2) + 1
    phase_index = harmonic_order[None, :] * (2 * sample_rows[:, None] + 1) % (4 * NT)
    phase_angle = phase_index.astype(jnp.float32) * (jnp.pi / (2 * NT))
    return jnp.where(column[None, :] % 2 == 0, jnp.cos(phase_angle), jnp.sin(phase_angle))


def per_sample(flags, value):
    return flags.reshape((-1,) + (1,) * (value.ndim - 1))


def digit_table(stages, count):
    found = {}
    for bits in itertools.product((0, 1), repeat=len(stages)):
        found.setdefault(sum(b * s for b, s in zip(bits, stages)) % count, bits)
    return np.array([found[d] for d in range(count)], np.int32)


def barrel(value, amounts, stages, axis):
    count = lax.axis_size(axis)
    picks = jnp.take(jnp.asarray(digit_table(stages, count)), amounts % count, axis=0)
    for level, steps in enumerate(stages):
        moved = shifted(value, axis, steps)
        value = jnp.where(per_sample(picks[:, level] == 1, value), moved, value)
    return value


def body(rotor_coeffs, mortar_weights, block_shifts, stencil_offsets, reluctivity, source):
    local_c, comp, _, nodes = rotor_coeffs.shape
    local_j, sten = mortar_weights.shape[:2]
    rows = nodes // LANES
    parts = lax.axis_size("tm")
    chunk = rows // parts
    coeffs = lax.all_to_all(
        rotor_coeffs.reshape(local_c, comp, rows, LANES), "tm", split_axis=2, concat_axis=0, tiled=True
    )
    weights = lax.all_to_all(
        mortar_weights.reshape(local_j, sten, rows, LANES), "tm", split_axis=2, concat_axis=0, tiled=True
    )
    small = jnp.concatenate([block_shifts[:, None], stencil_offsets], axis=1).astype(jnp.float32)
    small = lax.all_gather(small, "tm", tiled=True).astype(jnp.int32)
    shifts, offsets = small[:, 0], small[:, 1:]
    gain = lax.dynamic_slice_in_dim(
        reluctivity.reshape(rows, LANES), lax.axis_index("tm") * chunk, chunk, axis=0
    )
    table = harmonic_basis(jnp.arange(NT, dtype=jnp.int32), KC)
    samples = jnp.einsum("jc,capk->japk", table, coeffs, precision=lax.Precision.HIGHEST)
    orders = ((1, 2, 4, -8, 16), (16, 8, -4, 2, 1))
    fields = []
    for component in range(comp):
        turned = barrel(samples[:, component], shifts, orders[component % 2], "azim")
        from_left = shifted(turned, "azim", 1)
        from_right = shifted(turned, "azim", -1)
        field = jnp.zeros_like(turned)
        for stencil_entry in range(sten):
            offset = offsets[:, stencil_entry]
            neighbour = jnp.where(
                per_sample(offset == 0, turned),
                turned,
                jnp.where(per_sample(offset > 0, turned), from_right, from_left),
            )
            field = field + weights[:, stencil_entry] * neighbour
        fields.append(field)
    airgap_field = jnp.stack(fields, axis=1)
    square = jnp.sum(airgap_field * airgap_field, axis=1, keepdims=True)
    field_flux = gain[None, None] * (1.0 + square / (1.0 + square)) * airgap_field
    summed = jnp.einsum(
        "jc,japk->capk", table * (2.0 / NT), field_flux, precision=lax.Precision.HIGHEST
    )
    residual = lax.all_to_all(summed, "tm", split_axis=0, concat_axis=2, tiled=True)
    return residual.reshape(source.shape) - source


def solution(mesh):
    in_specs = (
        P("tm", None, "azim", None),
        P("tm", None, "azim", None),
        P("tm"),
        P("tm", None),
        P("azim", None),
        P("tm", None, "azim", None),
    )
    out_specs = P("tm", None, "azim", None)
    return jax.shard_map(body, mesh=mesh, in_specs=in_specs, out_specs=out_specs, check_vma=False)
```
